256 devices in a mesh: seq: 64 (over z, x, y_lo), head: 4 (over y_hi, core).
Axes of the slice: x: 4, y: 4 (y_hi: 2, y_lo: 2; y = y_hi * 2 + y_lo), z: 8, core: 2. Of those that a mesh axis runs over, the one named last changes fastest.
Arguments:
- query: bfloat16 [8192, 3072], P('seq', 'head'), may hold values from -256 to 256
- keys: bfloat16 [8192, 3072], P('seq', 'head'), may hold values from -4 to 4
- values: bfloat16 [8192, 3072], P('seq', 'head'), may hold values from -5 to 5
- out_weight: bfloat16 [3072, 4096], P('head'), may hold values from -0.109375 to 0.109375
- image_start: int32 [3], replicated, may hold values from 0 to 7168, as said below
Outputs:
- mixed: bfloat16 [8192, 4096], P('seq', 'head')
The draws below stay inside these ranges and needn't reach their ends.
Inputs may be any that keep to these rules, and one draw needn't show every extreme that they name: `image_start`: the starts increase; each image's 1024 positions lie inside the sequence and no two images share a position; the last image ends at the sequence's end.
All inputs are finite; a program needn't handle non-finite values.
Results may differ from the reference program's by a relative error of at most 0.012.
Values may be sent and summed in bfloat16 or wider, within the bound.
A program may use at most 192 MiB of HBM per device.

```python
import jax
import jax.numpy as jnp
from jax import lax

D = 4096
HEADS = 24
HEAD_DIM = 128
IMAGES = 3
TOKENS = 8192
PATCHES = 1024


def draw_keys(key, part):
    return jnp.clip(jax.random.normal(jax.random.fold_in(key, 3), (TOKENS, HEADS * HEAD_DIM), jnp.float32), -4.0, 4.0).astype(jnp.bfloat16)


def draw_query(key, part):
    return jnp.clip(jax.random.normal(jax.random.fold_in(key, 5), (TOKENS, HEADS * HEAD_DIM), jnp.float32), -4.0, 4.0).astype(jnp.bfloat16)


def draw_image_start(key, part):
    spare = TOKENS - IMAGES * PATCHES
    cuts = jnp.sort(jax.random.randint(jax.random.fold_in(key, 9), (IMAGES,), 0, spare + 1))
    cuts = cuts.at[IMAGES - 1].set(spare)
    return (cuts + jnp.arange(IMAGES, dtype=jnp.int32) * PATCHES).astype(jnp.int32)


def block_levels(key, extent, split, smallest, high):
    def one(dim, parts):
        heights = jax.random.uniform(jax.random.fold_in(jax.random.fold_in(key, 6), dim), (parts,), jnp.float32, smallest / len(split), high / len(split))
        return jnp.repeat(jnp.exp(heights), extent[dim] // parts).reshape((-1,) + (1,) * (len(extent) - dim - 1))

    factor_of = one(*split[0])
    for cut in split[1:]:
        factor_of = factor_of * one(*cut)
    return factor_of


def noise(own_key, shape, deviation, most, split=(), held_as=jnp.bfloat16):
    values = deviation * jax.random.normal(own_key, shape, jnp.float32)
    if split:
        values = values * block_levels(own_key, shape, split, -0.22, 0.18)
    return jnp.clip(values, -most, most).astype(held_as)


def setup_inputs(seed: int = 0) -> dict:
    streams_of = jax.random.split(jax.random.key(seed), 6)
    query = draw_query(jax.random.fold_in(streams_of[5], 71), 0)
    keys = draw_keys(jax.random.fold_in(streams_of[5], 71), 0)
    values = noise(streams_of[2], (TOKENS, HEADS * HEAD_DIM), 1.0, 5.0, ((0, 64), (1, 4)))
    out_weight = noise(streams_of[3], (HEADS * HEAD_DIM, D), (HEADS * HEAD_DIM) ** -0.5, 0.109375, ((0, 4),))
    image_start = draw_image_start(jax.random.fold_in(streams_of[5], 71), 0)
    return dict(query=query, keys=keys, values=values, out_weight=out_weight, image_start=image_start)


def image_tags(positions, image_start):
    inside = (positions[:, None] >= image_start[None, :]) & (positions[:, None] < image_start[None, :] + PATCHES)
    labels = jnp.arange(IMAGES, dtype=jnp.int32) + 1
    return jnp.sum(jnp.where(inside, labels[None, :], 0), axis=1).astype(jnp.int32) - 1


def reference(query, keys, values, out_weight, image_start):
    seq_total = query.shape[0]
    head_count = query.shape[1] // HEAD_DIM
    positions = jnp.arange(seq_total, dtype=jnp.int32)
    tags = image_tags(positions, image_start)
    key_heads = keys.reshape(seq_total, head_count, HEAD_DIM).astype(jnp.float32)
    value_heads = values.reshape(seq_total, head_count, HEAD_DIM).astype(jnp.float32)
    block_rows = min(512, seq_total)
    block_count = seq_total // block_rows
    query_blocks = query.reshape(block_count, block_rows, head_count, HEAD_DIM)
    scale = HEAD_DIM ** -0.5

    def attend(index):
        query_block = lax.dynamic_index_in_dim(query_blocks, index, 0, keepdims=False).astype(jnp.float32)
        query_pos = index * block_rows + jnp.arange(block_rows, dtype=jnp.int32)
        query_tag = lax.dynamic_slice_in_dim(tags, index * block_rows, block_rows)
        visible = (positions[None, :] <= query_pos[:, None]) | ((query_tag[:, None] == tags[None, :]) & (query_tag[:, None] >= 0))
        scores = jnp.einsum('qhd,khd->hqk', query_block, key_heads) * scale
        scores = jnp.where(visible[None], scores, -jnp.inf)
        row_max = jnp.max(scores, axis=-1, keepdims=True)
        weights = jnp.where(visible[None], jnp.exp(scores - row_max), 0.0)
        denominators = jnp.sum(weights, axis=-1)
        rounded = lax.optimization_barrier(weights.astype(jnp.bfloat16)).astype(jnp.float32)
        weighted = jnp.einsum('hqk,khd->qhd', rounded, value_heads)
        result = weighted / jnp.transpose(denominators)[:, :, None]
        return result.astype(jnp.bfloat16).reshape(block_rows, head_count * HEAD_DIM)

    attended = lax.map(attend, jnp.arange(block_count, dtype=jnp.int32))
    attended = attended.reshape(seq_total, head_count * HEAD_DIM)
    return jnp.dot(attended, out_weight, preferred_element_type=jnp.float32).astype(jnp.bfloat16)
```

```python
import math

import jax
import jax.numpy as jnp
from jax import lax
from jax.experimental import pallas as pl
from jax.experimental.pallas import tpu as pltpu
from jax.sharding import PartitionSpec as P

MESH = pl.DeviceIdType.MESH
HD = 128
PATCHES = 1024
NEG = -1e30
SCALE = HD**-0.5 * math.log2(math.e)


def place():
    s, h = lax.axis_index("seq"), lax.axis_index("head")
    return s // 8, (s // 2) % 4, s % 2, h // 2, h % 2


def device(z, x, yl, yh, c):
    return ((z * 4 + x) * 2 + yl, yh * 2 + c)


def kernel(
    start_ref, q_ref, k_ref, v_ref, w_ref, o_ref,
    vt, kv, qb, accs, ms, ls, lims, ot, att_t, att, wv, own, pair_out, pair_in, cross_out, cross_in,
    a_send, a_kv, a_q, x_send, x_recv, f_send, f_recv, p_send, p_recv, o_send, o_recv, w_sem, r_send, r_recv,
):
    z, x, yl, yh, c = place()
    active = z % 4 != 3
    home_core = z // 4
    head = 2 * (z % 4) + yl
    right, left = (x + 1) % 4, (x + 3) % 4
    opposite = (x + 2) % 4
    to_right = device(z, right, yl, yh, c)
    to_left = device(z, left, yl, yh, c)
    to_pair = device(z, x, yl, yh, 1 - c)
    to_cross = device(z, x, yl, 1 - yh, c)

    def worker(i):
        return 4 * c + i // 2, i % 2

    def is_own(i):
        wz, wyl = worker(i)
        return (wz == z) & (wyl == yl) & (yl == c)

    def source_is_own(zs):
        return (zs == z) & (yl == c) & (home_core == c)

    barrier = pltpu.get_barrier_semaphore()

    def greet(dev):
        pl.semaphore_signal(barrier, inc=1, device_id=dev, device_id_type=MESH)

    def greet_worker(i, _):
        wz, wyl = worker(i)

        @pl.when(jnp.logical_not(is_own(i)))
        def _():
            greet(device(wz, x, wyl, yh, yl))

        return 0

    lax.fori_loop(0, 6, greet_worker, 0)
    greet(to_pair)
    greet(to_cross)

    @pl.when(active)
    def _():
        greet(to_right)
        greet(to_left)

        def greet_source(zs, _):
            @pl.when(jnp.logical_not(source_is_own(zs)))
            def _():
                greet(device(zs, x, c, yh, home_core))

            return 0

        lax.fori_loop(0, 8, greet_source, 0)

    w_copy = pltpu.make_async_copy(w_ref, wv, w_sem)
    w_copy.start()
    for i in range(6):
        vt[i] = v_ref[:, i * HD : (i + 1) * HD].T
    for zq in range(8):
        pos = ((zq * 4 + x) * 2 + c) * HD + lax.broadcasted_iota(jnp.int32, (1, HD), 1)
        lim = pos
        for n in range(3):
            first = start_ref[n]
            lim = jnp.where((pos >= first) & (pos < first + PATCHES), first + (PATCHES - 1), lim)
        lims[zq] = jnp.broadcast_to(lim, (8, HD))

    own_pair = ((yl == c) & (home_core == c) & active).astype(jnp.int32)
    expected = 8 + jnp.where(active, 10, 0) - 2 * own_pair
    pl.semaphore_wait(barrier, expected)

    slot = (z * 4 + x) * 2 + yl

    def pieces(i):
        columns = pl.ds(i * HD, HD)
        return (
            (k_ref.at[:, columns], kv.at[0, slot], a_kv.at[z]),
            (vt.at[i], kv.at[1, slot], a_kv.at[z]),
            (q_ref.at[:, columns], qb.at[z], a_q.at[z]),
        )

    def a_copy(i, n):
        wz, wyl = worker(i)
        src, dst, sem = pieces(i)[n]
        return pltpu.make_async_remote_copy(
            src, dst, a_send.at[n, i], sem, device_id=device(wz, x, wyl, yh, yl), device_id_type=MESH
        )

    def a_local(i, n):
        src, dst, sem = pieces(i)[n]
        return pltpu.make_async_copy(src, dst, sem)

    def a_start(i, ns):
        @pl.when(is_own(i))
        def _():
            for n in ns:
                a_local(i, n).start()

        @pl.when(jnp.logical_not(is_own(i)))
        def _():
            for n in ns:
                a_copy(i, n).start()

    for i in range(6):
        a_start(i, (0, 1))
    for i in range(6):
        a_start(i, (2,))

    @pl.when(active)
    def _():
        def at(zk, xk, w):
            return (zk * 4 + xk) * 2 + w

        def nearest(d):
            off = jnp.where(d % 2 == 1, (d + 1) // 2, 8 - d // 2)
            return (z + off) % 8

        def x_copy(side, b):
            s = at(b, x, c)
            return pltpu.make_async_remote_copy(
                kv.at[:, s], kv.at[:, s], x_send.at[side, b], x_recv.at[side, b],
                device_id=to_right if side == 0 else to_left, device_id_type=MESH,
            )

        def x_wait(side, b):
            s = at(b, left if side == 0 else right, c)
            pltpu.make_async_remote_copy(
                kv.at[:, s], kv.at[:, s], x_send.at[side, b], x_recv.at[side, b],
                device_id=to_right if side == 0 else to_left, device_id_type=MESH,
            ).wait_recv()

        def f_copy(side, b):
            s = at(b, left if side == 0 else right, c)
            return pltpu.make_async_remote_copy(
                kv.at[side, s], kv.at[side, s], f_send.at[side, b], f_recv.at[side, b],
                device_id=to_right if side == 0 else to_left, device_id_type=MESH,
            )

        def f_wait(side, b):
            s = at(b, opposite, c)
            pltpu.make_async_remote_copy(
                kv.at[side, s], kv.at[side, s], f_send.at[side, b], f_recv.at[side, b],
                device_id=to_right if side == 0 else to_left, device_id_type=MESH,
            ).wait_recv()

        def p_copy(rel, b, w):
            s = at(b, (x + rel) % 4, w)
            return pltpu.make_async_remote_copy(
                kv.at[:, s], kv.at[:, s], p_send.at[rel, b], p_recv.at[rel, b], device_id=to_pair, device_id_type=MESH
            )

        def own_step(d, _):
            b = nearest(d)
            s = at(b, x, c)
            pltpu.make_async_remote_copy(
                kv.at[:, s], kv.at[:, s], x_send.at[0, b], a_kv.at[b], device_id=to_pair, device_id_type=MESH
            ).wait_recv()
            x_copy(0, b).start()
            x_copy(1, b).start()
            p_copy(0, b, c).start()
            return 0

        def side_step(d, _):
            b = nearest(d)
            x_wait(0, b)
            f_copy(0, b).start()
            p_copy(3, b, c).start()
            x_wait(1, b)
            f_copy(1, b).start()
            p_copy(1, b, c).start()
            return 0

        def far_step(d, _):
            b = nearest(d)
            f_wait(0, b)
            f_wait(1, b)
            p_copy(2, b, c).start()
            return 0

        def pair_wait(rel):
            def step(b, _):
                p_copy(rel, b, 1 - c).wait_recv()
                return 0

            lax.fori_loop(0, 8, step, 0)

        def q_wait(b, _):
            pltpu.make_async_remote_copy(
                qb.at[b], qb.at[b], x_send.at[0, b], a_q.at[b], device_id=to_pair, device_id_type=MESH
            ).wait_recv()
            return 0

        rows = lax.broadcasted_iota(jnp.int32, (4 * HD, HD), 0)
        rows = jnp.where(rows >= 2 * HD, rows + (8 * HD - 2 * HD), rows)

        def attend(xk, zq, carry, masked):
            def step(n, carry):
                m, l, acc = carry
                s0 = at(2 * n, xk, 0)
                k = jnp.concatenate([kv[0, s0], kv[0, s0 + 1], kv[0, s0 + 8], kv[0, s0 + 9]], axis=0)
                v = jnp.concatenate([kv[1, s0], kv[1, s0 + 1], kv[1, s0 + 8], kv[1, s0 + 9]], axis=1)
                sc = lax.dot_general(k, qb[zq], (((1,), (1,)), ((), ())), preferred_element_type=jnp.float32) * SCALE
                if masked:
                    sc = jnp.where(rows <= lims[zq, 0:1] - s0 * HD, sc, NEG)
                m_new = jnp.maximum(m, jnp.max(sc, axis=0, keepdims=True))
                p = jnp.exp2(sc - m_new)
                alpha = jnp.exp2(m - m_new)
                l = l * alpha + jnp.sum(p, axis=0, keepdims=True)
                acc = acc * alpha + jnp.dot(v, p.astype(jnp.bfloat16), preferred_element_type=jnp.float32)
                return m_new, l, acc

            first = zq // 2
            if masked:
                return lax.fori_loop(first, jnp.minimum((zq + 1) // 2, 3) + 1, step, carry)
            return lax.fori_loop(0, first, step, carry)

        def stage(rels, last):
            def per_q(zq, _):
                carry = (ms[zq, 0:1], ls[zq, 0:1], accs[zq])
                for rel in rels:
                    xk = (x + rel) % 4
                    carry = attend(xk, zq, carry, False)
                    carry = attend(xk, zq, carry, True)
                m, l, acc = carry
                if last:
                    ot[zq] = (acc * (1.0 / l)).astype(jnp.bfloat16)
                    own_source = source_is_own(zq)

                    @pl.when(own_source)
                    def _():
                        pltpu.make_async_copy(ot.at[zq], att_t.at[head], o_recv.at[head]).start()

                    @pl.when(jnp.logical_not(own_source))
                    def _():
                        o_copy(zq).start()
                else:
                    ms[zq] = jnp.broadcast_to(m, (8, HD))
                    ls[zq] = jnp.broadcast_to(l, (8, HD))
                    accs[zq] = acc
                return 0

            lax.fori_loop(0, 8, per_q, 0)

        def o_copy(zq):
            return pltpu.make_async_remote_copy(
                ot.at[zq], att_t.at[head], o_send.at[zq], o_recv.at[head],
                device_id=device(zq, x, c, yh, home_core), device_id_type=MESH,
            )

        ms[...] = jnp.full_like(ms, NEG)
        ls[...] = jnp.zeros_like(ls)
        accs[...] = jnp.zeros_like(accs)
        lax.fori_loop(0, 8, own_step, 0)
        lax.fori_loop(0, 8, q_wait, 0)
        lax.fori_loop(0, 8, side_step, 0)
        pair_wait(0)
        stage((0,), False)
        lax.fori_loop(0, 8, far_step, 0)
        pair_wait(3)
        pair_wait(1)
        stage((3, 1), False)
        pair_wait(2)
        stage((2,), True)

        def drain(b, _):
            for side in (0, 1):
                x_copy(side, b).wait_send()
                f_copy(side, b).wait_send()
            for rel in range(4):
                p_copy(rel, b, c).wait_send()

            @pl.when(jnp.logical_not(source_is_own(b)))
            def _():
                o_copy(b).wait_send()

            return 0

        lax.fori_loop(0, 8, drain, 0)

    for i in range(6):
        pltpu.make_async_remote_copy(
            att_t.at[i], att_t.at[i], a_send.at[0, i], o_recv.at[i], device_id=to_pair, device_id_type=MESH
        ).wait_recv()
        att[:, i * HD : (i + 1) * HD] = att_t[i].T

    w_copy.wait()
    width = o_ref.shape[1]

    def project(gy, gc):
        first = pl.multiple_of((gy * 2 + gc) * width, width)
        return jnp.dot(att[...], wv[:, pl.ds(first, width)], preferred_element_type=jnp.float32)

    def pair_copy(n):
        return pltpu.make_async_remote_copy(
            pair_out.at[n], pair_in.at[n], r_send.at[n], r_recv.at[n], device_id=to_pair, device_id_type=MESH
        )

    cross = pltpu.make_async_remote_copy(
        cross_out, cross_in, r_send.at[2], r_recv.at[2], device_id=to_cross, device_id_type=MESH
    )
    pair_out[0] = project(1 - yh, 1 - c).astype(jnp.bfloat16)
    pair_copy(0).start()
    own[...] = project(1 - yh, c)
    pair_copy(0).wait_recv()
    cross_out[...] = (own[...] + pair_in[0].astype(jnp.float32)).astype(jnp.bfloat16)
    cross.start()
    pair_out[1] = project(yh, 1 - c).astype(jnp.bfloat16)
    pair_copy(1).start()
    own[...] = project(yh, c)
    pair_copy(1).wait_recv()
    own[...] += pair_in[1].astype(jnp.float32)
    cross.wait_recv()
    o_ref[...] = (own[...] + cross_in[...].astype(jnp.float32)).astype(jnp.bfloat16)
    pair_copy(0).wait_send()
    pair_copy(1).wait_send()
    cross.wait_send()
    for i in range(6):

        @pl.when(jnp.logical_not(is_own(i)))
        def _():
            for n in range(3):
                a_copy(i, n).wait_send()


def body(query, keys, values, out_weight, image_start):
    rows, depth = query.shape
    width = out_weight.shape[1] // lax.axis_size("head")
    bf, f32, dma = jnp.bfloat16, jnp.float32, pltpu.SemaphoreType.DMA
    vmem = pl.BlockSpec(memory_space=pltpu.VMEM)
    return pl.pallas_call(
        kernel,
        out_shape=jax.ShapeDtypeStruct((rows, width), bf),
        in_specs=[pl.BlockSpec(memory_space=pltpu.SMEM), vmem, vmem, vmem, pl.BlockSpec(memory_space=pl.ANY)],
        out_specs=vmem,
        scratch_shapes=[
            pltpu.VMEM((6, HD, HD), bf),
            pltpu.VMEM((2, 64, HD, HD), bf),
            pltpu.VMEM((8, HD, HD), bf),
            pltpu.VMEM((8, HD, HD), f32),
            pltpu.VMEM((8, 8, HD), f32),
            pltpu.VMEM((8, 8, HD), f32),
            pltpu.VMEM((8, 8, HD), jnp.int32),
            pltpu.VMEM((8, HD, HD), bf),
            pltpu.VMEM((6, HD, HD), bf),
            pltpu.VMEM((rows, depth), bf),
            pltpu.VMEM(out_weight.shape, bf),
            pltpu.VMEM((rows, width), f32),
            pltpu.VMEM((2, rows, width), bf),
            pltpu.VMEM((2, rows, width), bf),
            pltpu.VMEM((rows, width), bf),
            pltpu.VMEM((rows, width), bf),
            dma((3, 6)), dma((8,)), dma((8,)), dma((2, 8)), dma((2, 8)), dma((2, 8)), dma((2, 8)),
            dma((4, 8)), dma((4, 8)), dma((8,)), dma((6,)), dma, dma((3,)), dma((3,)),
        ],
        compiler_params=pltpu.CompilerParams(
            collective_id=0, has_side_effects=True, vmem_limit_bytes=48 * 1024 * 1024
        ),
    )(image_start, query, keys, values, out_weight)


def solution(mesh):
    placed = (P("seq", "head"), P("seq", "head"), P("seq", "head"), P("head", None), P())
    return jax.shard_map(body, mesh=mesh, in_specs=placed, out_specs=P("seq", "head"), check_vma=False)
```

```python
import jax
import jax.numpy as jnp
from jax import lax
from jax.experimental import pallas as pl
from jax.experimental.pallas import tpu as pltpu
from jax.sharding import PartitionSpec as P

MESH = pl.DeviceIdType.MESH
HD = 128
PATCHES = 1024
NEG = -1e30
SCALE = HD**-0.5
PARTS = 2

BY_QUERY = [(t, z) for t in range(4) for z in range(min(2 * t + 3, 8))]
BY_KEY = [(t, z) for z in range(8) for t in range(4) if z <= 2 * t + 2]
UNITS = [(t, z, 0) for t, z in BY_QUERY] + [(t, z, r) for t, z in BY_KEY for r in (3, 1)] + [(t, z, 2) for t, z in BY_QUERY]
LOOPS = len(UNITS) // 2
WINDOW = 3


def first_use(first, last):
    seen = {}
    for u in range(first, last):
        seen.setdefault(UNITS[u][1], u // 2)
    plan = {}
    for z, i in sorted(seen.items(), reverse=True):
        while i in plan:
            i -= 1
        plan[i] = z
    return {i: z for i, z in plan.items() if i > 0}


TODO = (
    {},
    {3: 4, 6: 5},
    {2: 0, 4: 1, 8: 2, 11: 3, 14: 4, 18: 5},
    first_use(0, 23),
    first_use(23, 69),
    first_use(69, 92),
    {1: 1, 4: 2, 7: 3},
    {37: 0, 40: 1, 43: 2},
)


def place():
    s, h = lax.axis_index("seq"), lax.axis_index("head")
    return s // 8, (s // 2) % 4, s % 2, h // 2, h % 2


def device(z, x, yl, yh, c):
    return ((z * 4 + x) * 2 + yl, yh * 2 + c)


def kernel(
    start_hbm, q_hbm, k_hbm, v_hbm, w_ref, o_ref,
    start_ref, todo, q_ref, k_ref, v_ref, vt, kv, qb, accs, ms, lims, ot, att, wv, own, pair_out, pair_in, cross_out, cross_in,
    s0, s1, p0, p1, al0, al1,
    in_sem, a_send, a_kv, a_q, x_send, x_recv, f_send, f_recv, p_send, p_recv, o_send, o_recv, w_sem,
    pair_send, pair_recv, cross_send, cross_recv,
):
    bf, f32 = jnp.bfloat16, jnp.float32
    z, x, yl, yh, c = place()
    couple = z // 2
    active = (z % 2 == 0) | (yl == couple % 2)
    home_core = z // 4
    head = 3 * (couple % 2) + jnp.where(z % 2 == 1, 2, yl)
    right, left = (x + 1) % 4, (x + 3) % 4
    opposite = (x + 2) % 4
    to_right = device(z, right, yl, yh, c)
    to_left = device(z, left, yl, yh, c)
    to_pair = device(z, x, yl, yh, 1 - c)
    to_cross = device(z, x, yl, 1 - yh, c)

    def remote(src, dst, send, recv, dev):
        return pltpu.make_async_remote_copy(src, dst, send, recv, device_id=dev, device_id_type=MESH)

    def worker(i):
        k, j = 2 * c + i // 3, i % 3
        extra = j == 2
        return 2 * k + jnp.where(extra, 1, 0), jnp.where(extra, k % 2, j)

    def is_own(i):
        wz, wyl = worker(i)
        return (wz == z) & (wyl == yl) & (yl == c)

    def source_is_own(zs):
        return (zs == z) & (yl == c) & (home_core == c)

    def columns(i):
        return pl.ds(pl.multiple_of(i * HD, HD), HD)

    copies = [
        pltpu.make_async_copy(src, dst, in_sem.at[n])
        for n, (src, dst) in enumerate(
            ((v_hbm, v_ref), (k_hbm, k_ref), (q_hbm, q_ref), (start_hbm, start_ref))
        )
    ]
    for copy in copies:
        copy.start()

    barrier = pltpu.get_barrier_semaphore()

    def greet(dev):
        pl.semaphore_signal(barrier, inc=1, device_id=dev, device_id_type=MESH)

    def greet_worker(i, _):
        wz, wyl = worker(i)

        @pl.when(jnp.logical_not(is_own(i)))
        def _():
            greet(device(wz, x, wyl, yh, yl))

        return 0

    @pl.when(active)
    def _():
        def greet_source(n, _):
            zs = (z + 4 + n) % 8

            @pl.when(jnp.logical_not(source_is_own(zs)))
            def _():
                greet(device(zs, x, c, yh, home_core))

            return 0

        lax.fori_loop(0, 8, greet_source, 0)
        greet(to_right)
        greet(to_left)

    lax.fori_loop(0, 6, greet_worker, 0)
    greet(to_pair)
    greet(to_cross)

    w_copy = pltpu.make_async_copy(w_ref, wv, w_sem)
    copies[0].wait()
    for i in range(6):
        vt[i] = v_ref[:, i * HD : (i + 1) * HD].T
    for copy in copies[1:]:
        copy.wait()
    w_copy.start()

    def clear(n, _):
        todo[n] = -1
        return 0

    lax.fori_loop(0, len(TODO) * LOOPS, clear, 0)
    for k, plan in enumerate(TODO):
        for i, value in plan.items():
            todo[k * LOOPS + i] = value
            todo[i] = 0
    lanes = lax.broadcasted_iota(jnp.int32, (1, 2 * HD), 1)
    for t in range(4):
        zq = 2 * t + lanes // HD
        pos = ((zq * 4 + x) * 2 + c) * HD + lanes % HD
        lim = pos
        for n in range(3):
            first = start_ref[n]
            lim = jnp.where((pos >= first) & (pos < first + PATCHES), first + (PATCHES - 1), lim)
        lims[t] = jnp.broadcast_to(lim, (8, 2 * HD))
    ms[...] = jnp.full_like(ms, NEG)
    accs[...] = jnp.zeros_like(accs)

    own_pair = ((yl == c) & (home_core == c) & active).astype(jnp.int32)
    expected = 8 + jnp.where(active, 10, 0) - 2 * own_pair
    pl.semaphore_wait(barrier, expected)

    slot = (z * 4 + x) * 2 + yl

    def pieces(i):
        return (
            (k_ref.at[:, columns(i)], kv.at[0, slot], a_kv.at[z]),
            (vt.at[i], kv.at[1, slot], a_kv.at[z]),
            (q_ref.at[:, columns(i)], qb.at[z], a_q.at[z]),
        )

    def a_copy(i, n):
        wz, wyl = worker(i)
        src, dst, sem = pieces(i)[n]
        return remote(src, dst, a_send.at[n, i], sem, device(wz, x, wyl, yh, yl))

    def a_start(i):
        @pl.when(is_own(i))
        def _():
            for src, dst, sem in pieces(i):
                pltpu.make_async_copy(src, dst, sem).start()

        @pl.when(jnp.logical_not(is_own(i)))
        def _():
            for n in range(3):
                a_copy(i, n).start()

    def a_sent(i):
        @pl.when(jnp.logical_not(is_own(i)))
        def _():
            for n in range(3):
                a_copy(i, n).wait_send()

    def a_round(m):
        @pl.when(m < 6)
        def _():
            @pl.when(m >= WINDOW)
            def _():
                a_sent((m - WINDOW + z) % 6)

            a_start((m + z) % 6)

    @pl.when(jnp.logical_not(active))
    def _():
        def step(m, _):
            a_round(m)
            return 0

        lax.fori_loop(0, 6, step, 0)

    @pl.when(active)
    def _():
        def at(zk, xk, w):
            return (zk * 4 + xk) * 2 + w

        def x_copy(side, b):
            s = at(b, x, c)
            return remote(
                kv.at[:, s], kv.at[:, s], x_send.at[side, b], x_recv.at[side, b], to_right if side == 0 else to_left
            )

        def x_wait(side, b):
            s = at(b, left if side == 0 else right, c)
            remote(
                kv.at[:, s], kv.at[:, s], x_send.at[side, b], x_recv.at[side, b], to_right if side == 0 else to_left
            ).wait_recv()

        def f_copy(side, b):
            s = at(b, left if side == 0 else right, c)
            return remote(
                kv.at[side, s], kv.at[side, s], f_send.at[side, b], f_recv.at[side, b],
                to_right if side == 0 else to_left,
            )

        def f_wait(side, b):
            s = at(b, opposite, c)
            remote(
                kv.at[side, s], kv.at[side, s], f_send.at[side, b], f_recv.at[side, b],
                to_right if side == 0 else to_left,
            ).wait_recv()

        def p_copy(rel, b, w):
            s = at(b, (x + rel) % 4, w)
            return remote(kv.at[:, s], kv.at[:, s], p_send.at[rel, b], p_recv.at[rel, b], to_pair)

        def o_copy(zq):
            return remote(
                ot.at[zq], att.at[:, columns(head)], o_send.at[zq], o_recv.at[head],
                device(zq, x, c, yh, home_core),
            )

        def own_step(b):
            s = at(b, x, c)
            remote(kv.at[:, s], kv.at[:, s], x_send.at[0, b], a_kv.at[b], to_pair).wait_recv()
            x_copy(0, b).start()
            x_copy(1, b).start()
            p_copy(0, b, c).start()

        def side_step(b):
            x_wait(0, b)
            f_copy(0, b).start()
            p_copy(3, b, c).start()
            x_wait(1, b)
            f_copy(1, b).start()
            p_copy(1, b, c).start()

        def far_step(b):
            f_wait(0, b)
            f_wait(1, b)
            p_copy(2, b, c).start()

        def q_wait(t):
            for b in (2 * t, 2 * t + 1):
                remote(qb.at[b], qb.at[b], x_send.at[0, b], a_q.at[b], to_pair).wait_recv()

        scores, weights, scales = (s0, s1), (p0, p1), (al0, al1)
        rows = lax.broadcasted_iota(jnp.int32, (2 * HD, 2 * HD), 0)
        ones = jnp.ones((16, 2 * HD), bf)

        def score(t, b, n):
            k = kv[0, pl.ds(b, 2)].reshape(2 * HD, HD)
            q = qb[pl.ds(2 * t, 2)].reshape(2 * HD, HD)
            scores[n][...] = lax.dot_general(k, q, (((1,), (1,)), ((), ())), preferred_element_type=f32)

        def weigh(t, b, n):
            sc = jnp.where(rows <= lims[t, 0:1] - b * HD, scores[n][...], NEG)
            m = ms[t, 0:1]
            m_new = jnp.maximum(m, jnp.max(sc, axis=0, keepdims=True))
            weights[n][...] = jnp.exp((sc - m_new) * SCALE).astype(bf)
            scales[n][...] = jnp.broadcast_to(jnp.exp((m - m_new) * SCALE), (8, 2 * HD))
            ms[t, 0:1] = m_new

        def gather(t, b, n):
            v = jnp.concatenate([jnp.concatenate([kv[1, b], kv[1, b + 1]], axis=1), ones], axis=0)
            accs[t] = accs[t] * scales[n][0:1] + jnp.dot(v, weights[n][...], preferred_element_type=f32)

        def finish(t):
            total = accs[t]
            done = total[:HD] * (1.0 / total[HD : HD + 1])
            for j in range(2):
                zq = 2 * t + j
                ot[zq] = done[:, j * HD : (j + 1) * HD].T.astype(bf)

                @pl.when(source_is_own(zq))
                def _():
                    pltpu.make_async_copy(ot.at[zq], att.at[:, columns(head)], o_recv.at[head]).start()

                @pl.when(jnp.logical_not(source_is_own(zq)))
                def _():
                    o_copy(zq).start()

        def pair_wait(rels):
            def run(b):
                for rel in rels:
                    p_copy(rel, b, 1 - c).wait_recv()

            return run

        def in_round(step):
            def run(m):
                b = (head + 12 - m) % 6
                step(b)

                @pl.when(b < 2)
                def _():
                    step(b + 6)

            return run

        actions = (in_round(side_step), in_round(far_step), pair_wait((0,)), pair_wait((3, 1)), pair_wait((2,)), q_wait, finish)

        def events(i):
            @pl.when(todo[i] >= 0)
            def _():
                for k, action in enumerate(actions):
                    value = todo[(k + 1) * LOOPS + i]

                    @pl.when(value >= 0)
                    def _():
                        action(value)

        def steps(u, marks):
            n = jnp.int32(0)
            for mark in marks:
                n = n + (u >= mark).astype(jnp.int32)
            return n

        def unit(u):
            u = jnp.asarray(u, jnp.int32)
            by_query = (u < 23) | (u >= 69)
            v = jnp.where(u < 23, u, jnp.where(u < 69, (u - 23) // 2, u - 69))
            tq = steps(v, (3, 8, 15))
            zq = v - tq * (tq + 2)
            zk = steps(v, (4, 8, 12, 15, 18, 20, 22))
            skipped = steps(v, (15, 20, 22))
            low = steps(zk, (3, 5, 7))
            begin = 4 * zk - steps(zk, (4, 5, 6, 6, 7, 7))
            tk = low + v - begin
            rel = jnp.where(u < 23, 0, jnp.where(u >= 69, 2, jnp.where((u - 23) % 2 == 0, 3, 1)))
            t = jnp.where(by_query, tq, tk)
            zz = jnp.where(by_query, zq, zk)
            return t, zz, rel

        def look(u):
            t, zz, rel = unit(u)
            return t, at(zz, (x + rel) % 4, 0)

        for m in range(WINDOW - 1):
            a_round(jnp.int32(m))

        def first(m, _):
            a_round(m + (WINDOW - 1))
            in_round(own_step)(m)

            @pl.when(m >= 2)
            def _():
                in_round(side_step)(m - 2)

            return 0

        lax.fori_loop(0, 6, first, 0)
        q_wait(0)
        pair_wait((0,))(0)
        pair_wait((0,))(1)
        u0, u1 = look(0), look(1)
        score(*u0, 0)
        score(*u1, 1)
        weigh(*u0, 0)

        def two(i, _):
            events(i)
            before, last, now, later = [look(2 * i + n) for n in (-2, -1, 0, 1)]
            score(*now, 0)
            weigh(*last, 1)
            gather(*before, 0)
            score(*later, 1)
            weigh(*now, 0)
            gather(*last, 1)
            return 0

        lax.fori_loop(1, LOOPS, two, 0)
        before, last = look(2 * LOOPS - 2), look(2 * LOOPS - 1)
        weigh(*last, 1)
        gather(*before, 0)
        gather(*last, 1)
        finish(3)

    for i in range(6):
        remote(att.at[:, columns(i)], att.at[:, columns(i)], a_send.at[0, i], o_recv.at[i], to_pair).wait_recv()

    w_copy.wait()
    width = o_ref.shape[1]
    part = width // PARTS

    def project(gy, gc, p):
        first = pl.multiple_of((gy * 2 + gc) * width + p * part, part)
        return jnp.dot(att[...], wv[:, pl.ds(first, part)], preferred_element_type=f32)

    def pair_copy(n, p):
        return remote(pair_out.at[n, p], pair_in.at[n, p], pair_send.at[n, p], pair_recv.at[n, p], to_pair)

    def cross_copy(p):
        return remote(cross_out.at[p], cross_in.at[p], cross_send.at[p], cross_recv.at[p], to_cross)

    for p in range(PARTS):
        pair_out[0, p] = project(1 - yh, 1 - c, p).astype(bf)
        pair_copy(0, p).start()
    for p in range(PARTS):
        own[p] = project(1 - yh, c, p)
        pair_copy(0, p).wait_recv()
        cross_out[p] = (own[p] + pair_in[0, p].astype(f32)).astype(bf)
        cross_copy(p).start()
    for p in range(PARTS):
        pair_out[1, p] = project(yh, 1 - c, p).astype(bf)
        pair_copy(1, p).start()
    for p in range(PARTS):
        own[p] = project(yh, c, p)
        pair_copy(1, p).wait_recv()
        own[p] += pair_in[1, p].astype(f32)
    for p in range(PARTS):
        cross_copy(p).wait_recv()
        o_ref[:, p * part : (p + 1) * part] = (own[p] + cross_in[p].astype(f32)).astype(bf)

    for p in range(PARTS):
        pair_copy(0, p).wait_send()
        pair_copy(1, p).wait_send()
        cross_copy(p).wait_send()

    def a_drain(m, _):
        a_sent((m + z) % 6)
        return 0

    lax.fori_loop(6 - WINDOW, 6, a_drain, 0)

    @pl.when(active)
    def _():
        def drain(b, _):
            for side in (0, 1):
                s = (b * 4 + x) * 2 + c
                to = to_right if side == 0 else to_left
                remote(kv.at[:, s], kv.at[:, s], x_send.at[side, b], x_recv.at[side, b], to).wait_send()
                remote(kv.at[side, s], kv.at[side, s], f_send.at[side, b], f_recv.at[side, b], to).wait_send()
            for rel in range(4):
                s = (b * 4 + (x + rel) % 4) * 2 + c
                remote(kv.at[:, s], kv.at[:, s], p_send.at[rel, b], p_recv.at[rel, b], to_pair).wait_send()

            @pl.when(jnp.logical_not(source_is_own(b)))
            def _():
                remote(
                    ot.at[b], att.at[:, columns(head)], o_send.at[b], o_recv.at[head],
                    device(b, x, c, yh, home_core),
                ).wait_send()

            return 0

        lax.fori_loop(0, 8, drain, 0)


def body(query, keys, values, out_weight, image_start):
    rows, depth = query.shape
    width = out_weight.shape[1] // lax.axis_size("head")
    part = width // PARTS
    bf, f32, dma, hd = jnp.bfloat16, jnp.float32, pltpu.SemaphoreType.DMA, HD
    return pl.pallas_call(
        kernel,
        out_shape=jax.ShapeDtypeStruct((rows, width), bf),
        in_specs=[pl.BlockSpec(memory_space=pl.ANY)] * 5,
        out_specs=pl.BlockSpec(memory_space=pltpu.VMEM),
        scratch_shapes=[
            pltpu.SMEM((3,), jnp.int32),
            pltpu.SMEM((len(TODO) * LOOPS,), jnp.int32),
            pltpu.VMEM((rows, depth), bf),
            pltpu.VMEM((rows, depth), bf),
            pltpu.VMEM((rows, depth), bf),
            pltpu.VMEM((6, hd, hd), bf),
            pltpu.VMEM((2, 64, hd, hd), bf),
            pltpu.VMEM((8, hd, hd), bf),
            pltpu.VMEM((4, hd + 16, 2 * hd), f32),
            pltpu.VMEM((4, 8, 2 * hd), f32),
            pltpu.VMEM((4, 8, 2 * hd), jnp.int32),
            pltpu.VMEM((8, hd, hd), bf),
            pltpu.VMEM((rows, depth), bf),
            pltpu.VMEM(out_weight.shape, bf),
            pltpu.VMEM((PARTS, rows, part), f32),
            pltpu.VMEM((2, PARTS, rows, part), bf),
            pltpu.VMEM((2, PARTS, rows, part), bf),
            pltpu.VMEM((PARTS, rows, part), bf),
            pltpu.VMEM((PARTS, rows, part), bf),
            pltpu.VMEM((2 * hd, 2 * hd), f32),
            pltpu.VMEM((2 * hd, 2 * hd), f32),
            pltpu.VMEM((2 * hd, 2 * hd), bf),
            pltpu.VMEM((2 * hd, 2 * hd), bf),
            pltpu.VMEM((8, 2 * hd), f32),
            pltpu.VMEM((8, 2 * hd), f32),
            dma((4,)), dma((3, 6)), dma((8,)), dma((8,)), dma((2, 8)), dma((2, 8)), dma((2, 8)), dma((2, 8)),
            dma((4, 8)), dma((4, 8)), dma((8,)), dma((6,)), dma,
            dma((2, PARTS)), dma((2, PARTS)), dma((PARTS,)), dma((PARTS,)),
        ],
        compiler_params=pltpu.CompilerParams(
            collective_id=0, has_side_effects=True, vmem_limit_bytes=48 * 1024 * 1024
        ),
    )(image_start, query, keys, values, out_weight)


def solution(mesh):
    placed = (P("seq", "head"), P("seq", "head"), P("seq", "head"), P("head", None), P())
    return jax.shard_map(body, mesh=mesh, in_specs=placed, out_specs=P("seq", "head"), check_vma=False)
```

```python
import jax
import jax.numpy as jnp
from jax import lax
from jax.experimental import pallas as pl
from jax.experimental.pallas import tpu as pltpu
from jax.sharding import PartitionSpec as P

MESH = pl.DeviceIdType.MESH
HD = 128
PATCHES = 1024
NEG = -1e30
SCALE = HD**-0.5
PARTS = 2

BY_QUERY = [(t, z) for t in range(4) for z in range(min(2 * t + 3, 8))]
BY_KEY = [(t, z) for z in range(8) for t in range(4) if z <= 2 * t + 2]
UNITS = [(t, z, 0) for t, z in BY_QUERY] + [(t, z, r) for t, z in BY_KEY for r in (3, 1)] + [(t, z, 2) for t, z in BY_QUERY]
LOOPS = len(UNITS) // 2
WINDOW = 4


def first_use(first, last):
    seen = {}
    for u in range(first, last):
        seen.setdefault(UNITS[u][1], u // 2)
    plan = {}
    for z, i in sorted(seen.items(), reverse=True):
        while i in plan:
            i -= 1
        plan[i] = z
    return {i: z for i, z in plan.items() if i > 0}


TODO = (
    {},
    {1: 0, 2: 1, 3: 2, 4: 3, 5: 4, 6: 5},
    {7: 0, 9: 1, 11: 2, 13: 3, 15: 4, 18: 5},
    first_use(0, 23),
    first_use(23, 69),
    first_use(69, 92),
    {1: 1, 4: 2, 7: 3},
    {37: 0, 40: 1, 43: 2},
)


def place():
    s, h = lax.axis_index("seq"), lax.axis_index("head")
    return s // 8, (s // 2) % 4, s % 2, h // 2, h % 2


def device(z, x, yl, yh, c):
    return ((z * 4 + x) * 2 + yl, yh * 2 + c)


def kernel(
    start_hbm, q_hbm, k_hbm, v_hbm, w_ref, o_ref,
    start_ref, todo, q_ref, k_ref, v_ref, vt, kv, qb, accs, ms, lims, ot, att, wv, own, pair_out, pair_in, cross_out, cross_in,
    s0, s1, p0, p1, al0, al1,
    in_sem, a_send, a_kv, a_q, x_send, x_recv, f_send, f_recv, p_send, p_recv, o_send, o_recv, w_sem,
    pair_send, pair_recv, cross_send, cross_recv,
):
    bf, f32 = jnp.bfloat16, jnp.float32
    z, x, yl, yh, c = place()
    couple = z // 2
    active = (z % 2 == 0) | (yl == couple % 2)
    home_core = z // 4
    head = 3 * (couple % 2) + jnp.where(z % 2 == 1, 2, yl)
    right, left = (x + 1) % 4, (x + 3) % 4
    opposite = (x + 2) % 4
    to_right = device(z, right, yl, yh, c)
    to_left = device(z, left, yl, yh, c)
    to_pair = device(z, x, yl, yh, 1 - c)
    to_cross = device(z, x, yl, 1 - yh, c)

    def remote(src, dst, send, recv, dev):
        return pltpu.make_async_remote_copy(src, dst, send, recv, device_id=dev, device_id_type=MESH)

    def worker(i):
        k, j = 2 * c + i // 3, i % 3
        extra = j == 2
        return 2 * k + jnp.where(extra, 1, 0), jnp.where(extra, k % 2, j)

    def is_own(i):
        wz, wyl = worker(i)
        return (wz == z) & (wyl == yl) & (yl == c)

    def source_is_own(zs):
        return (zs == z) & (yl == c) & (home_core == c)

    def columns(i):
        return pl.ds(pl.multiple_of(i * HD, HD), HD)

    copies = [
        pltpu.make_async_copy(src, dst, in_sem.at[n])
        for n, (src, dst) in enumerate(
            ((v_hbm, v_ref), (k_hbm, k_ref), (q_hbm, q_ref), (start_hbm, start_ref))
        )
    ]
    for copy in copies:
        copy.start()

    barrier = pltpu.get_barrier_semaphore()

    def greet(dev):
        pl.semaphore_signal(barrier, inc=1, device_id=dev, device_id_type=MESH)

    def greet_worker(i, _):
        wz, wyl = worker(i)

        @pl.when(jnp.logical_not(is_own(i)))
        def _():
            greet(device(wz, x, wyl, yh, yl))

        return 0

    @pl.when(active)
    def _():
        def greet_source(n, _):
            zs = (z + 4 + n) % 8

            @pl.when(jnp.logical_not(source_is_own(zs)))
            def _():
                greet(device(zs, x, c, yh, home_core))

            return 0

        lax.fori_loop(0, 8, greet_source, 0)
        greet(to_right)
        greet(to_left)

    lax.fori_loop(0, 6, greet_worker, 0)
    greet(to_pair)
    greet(to_cross)

    w_copy = pltpu.make_async_copy(w_ref, wv, w_sem)
    copies[0].wait()
    for i in range(6):
        vt[i] = v_ref[:, i * HD : (i + 1) * HD].T
    for copy in copies[1:]:
        copy.wait()
    w_copy.start()

    own_pair = ((yl == c) & (home_core == c) & active).astype(jnp.int32)
    expected = 8 + jnp.where(active, 10, 0) - 2 * own_pair
    pl.semaphore_wait(barrier, expected)

    slot = (z * 4 + x) * 2 + yl

    def pieces(i):
        return (
            (k_ref.at[:, columns(i)], kv.at[0, slot], a_kv.at[z]),
            (vt.at[i], kv.at[1, slot], a_kv.at[z]),
            (q_ref.at[:, columns(i)], qb.at[z], a_q.at[z]),
        )

    def a_copy(i, n):
        wz, wyl = worker(i)
        src, dst, sem = pieces(i)[n]
        return remote(src, dst, a_send.at[n, i], sem, device(wz, x, wyl, yh, yl))

    def a_start(i, ns):
        @pl.when(is_own(i))
        def _():
            for n in ns:
                src, dst, sem = pieces(i)[n]
                pltpu.make_async_copy(src, dst, sem).start()

        @pl.when(jnp.logical_not(is_own(i)))
        def _():
            for n in ns:
                a_copy(i, n).start()

    def a_sent(i, ns):
        @pl.when(jnp.logical_not(is_own(i)))
        def _():
            for n in ns:
                a_copy(i, n).wait_send()

    def a_round(m):
        @pl.when(m < 6)
        def _():
            @pl.when(m >= WINDOW)
            def _():
                a_sent((m - WINDOW + z) % 6, (0, 1))

            a_start((m + z) % 6, (0, 1))

        @pl.when(m == 6)
        def _():
            def all_q(n, _):
                a_start((n + z) % 6, (2,))
                return 0

            lax.fori_loop(0, 6, all_q, 0)

    @pl.when(jnp.logical_not(active))
    def _():
        def step(m, _):
            a_round(m)
            return 0

        lax.fori_loop(0, 7, step, 0)

    @pl.when(active)
    def _():
        def at(zk, xk, w):
            return (zk * 4 + xk) * 2 + w

        def x_copy(side, b):
            s = at(b, x, c)
            return remote(
                kv.at[:, s], kv.at[:, s], x_send.at[side, b], x_recv.at[side, b], to_right if side == 0 else to_left
            )

        def x_wait(side, b):
            s = at(b, left if side == 0 else right, c)
            remote(
                kv.at[:, s], kv.at[:, s], x_send.at[side, b], x_recv.at[side, b], to_right if side == 0 else to_left
            ).wait_recv()

        def f_copy(side, b):
            s = at(b, left if side == 0 else right, c)
            return remote(
                kv.at[side, s], kv.at[side, s], f_send.at[side, b], f_recv.at[side, b],
                to_right if side == 0 else to_left,
            )

        def f_wait(side, b):
            s = at(b, opposite, c)
            remote(
                kv.at[side, s], kv.at[side, s], f_send.at[side, b], f_recv.at[side, b],
                to_right if side == 0 else to_left,
            ).wait_recv()

        def p_copy(rel, b, w):
            s = at(b, (x + rel) % 4, w)
            return remote(kv.at[:, s], kv.at[:, s], p_send.at[rel, b], p_recv.at[rel, b], to_pair)

        def o_copy(zq):
            return remote(
                ot.at[zq], att.at[:, columns(head)], o_send.at[zq], o_recv.at[head],
                device(zq, x, c, yh, home_core),
            )

        def own_step(b):
            s = at(b, x, c)
            remote(kv.at[:, s], kv.at[:, s], x_send.at[0, b], a_kv.at[b], to_pair).wait_recv()
            x_copy(0, b).start()
            x_copy(1, b).start()
            p_copy(0, b, c).start()

        def side_step(b):
            x_wait(0, b)
            f_copy(0, b).start()
            p_copy(3, b, c).start()
            x_wait(1, b)
            f_copy(1, b).start()
            p_copy(1, b, c).start()

        def far_step(b):
            f_wait(0, b)
            f_wait(1, b)
            p_copy(2, b, c).start()

        def q_wait(t):
            for b in (2 * t, 2 * t + 1):
                remote(qb.at[b], qb.at[b], x_send.at[0, b], a_q.at[b], to_pair).wait_recv()

        scores, weights, scales = (s0, s1), (p0, p1), (al0, al1)
        rows = lax.broadcasted_iota(jnp.int32, (2 * HD, 2 * HD), 0)
        ones = jnp.ones((16, 2 * HD), bf)

        def score(t, b, n):
            k = kv[0, pl.ds(b, 2)].reshape(2 * HD, HD)
            q = qb[pl.ds(2 * t, 2)].reshape(2 * HD, HD)
            scores[n][...] = lax.dot_general(k, q, (((1,), (1,)), ((), ())), preferred_element_type=f32)

        def weigh(t, b, n):
            sc = jnp.where(rows <= lims[t, 0:1] - b * HD, scores[n][...], NEG)
            m = ms[t, 0:1]
            m_new = jnp.maximum(m, jnp.max(sc, axis=0, keepdims=True))
            weights[n][...] = jnp.exp((sc - m_new) * SCALE).astype(bf)
            scales[n][...] = jnp.broadcast_to(jnp.exp((m - m_new) * SCALE), (8, 2 * HD))
            ms[t, 0:1] = m_new

        def gather(t, b, n):
            v = jnp.concatenate([jnp.concatenate([kv[1, b], kv[1, b + 1]], axis=1), ones], axis=0)
            accs[t] = accs[t] * scales[n][0:1] + jnp.dot(v, weights[n][...], preferred_element_type=f32)

        def finish(t):
            total = accs[t]
            done = total[:HD] * (1.0 / total[HD : HD + 1])
            for j in range(2):
                zq = 2 * t + j
                ot[zq] = done[:, j * HD : (j + 1) * HD].T.astype(bf)

                @pl.when(source_is_own(zq))
                def _():
                    pltpu.make_async_copy(ot.at[zq], att.at[:, columns(head)], o_recv.at[head]).start()

                @pl.when(jnp.logical_not(source_is_own(zq)))
                def _():
                    o_copy(zq).start()

        def pair_wait(rels):
            def run(b):
                for rel in rels:
                    p_copy(rel, b, 1 - c).wait_recv()

            return run

        def in_round(step):
            def run(m):
                b = (head + 12 - m) % 6
                step(b)

                @pl.when(b < 2)
                def _():
                    step(b + 6)

            return run

        actions = (in_round(side_step), in_round(far_step), pair_wait((0,)), pair_wait((3, 1)), pair_wait((2,)), q_wait, finish)

        def events(i):
            @pl.when(todo[i] >= 0)
            def _():
                for k, action in enumerate(actions):
                    value = todo[(k + 1) * LOOPS + i]

                    @pl.when(value >= 0)
                    def _():
                        action(value)

        def steps(u, marks):
            n = jnp.int32(0)
            for mark in marks:
                n = n + (u >= mark).astype(jnp.int32)
            return n

        def unit(u):
            u = jnp.asarray(u, jnp.int32)
            by_query = (u < 23) | (u >= 69)
            v = jnp.where(u < 23, u, jnp.where(u < 69, (u - 23) // 2, u - 69))
            tq = steps(v, (3, 8, 15))
            zq = v - tq * (tq + 2)
            zk = steps(v, (4, 8, 12, 15, 18, 20, 22))
            skipped = steps(v, (15, 20, 22))
            low = steps(zk, (3, 5, 7))
            begin = 4 * zk - steps(zk, (4, 5, 6, 6, 7, 7))
            tk = low + v - begin
            rel = jnp.where(u < 23, 0, jnp.where(u >= 69, 2, jnp.where((u - 23) % 2 == 0, 3, 1)))
            t = jnp.where(by_query, tq, tk)
            zz = jnp.where(by_query, zq, zk)
            return t, zz, rel

        def look(u):
            t, zz, rel = unit(u)
            return t, at(zz, (x + rel) % 4, 0)

        for m in range(WINDOW - 1):
            a_round(jnp.int32(m))

        def clear(n, _):
            for k in range(len(TODO)):
                todo[k * LOOPS + n] = -1
            return 0

        lax.fori_loop(0, LOOPS, clear, 0)
        for k, plan in enumerate(TODO):
            for i, value in plan.items():
                todo[k * LOOPS + i] = value
                todo[i] = 0
        lanes = lax.broadcasted_iota(jnp.int32, (1, 2 * HD), 1)
        for t in range(4):
            zq = 2 * t + lanes // HD
            pos = ((zq * 4 + x) * 2 + c) * HD + lanes % HD
            lim = pos
            for n in range(3):
                first = start_ref[n]
                lim = jnp.where((pos >= first) & (pos < first + PATCHES), first + (PATCHES - 1), lim)
            lims[t] = jnp.broadcast_to(lim, (8, 2 * HD))
        ms[...] = jnp.full_like(ms, NEG)
        accs[...] = jnp.zeros_like(accs)

        def first(m, _):
            a_round(m + (WINDOW - 1))
            in_round(own_step)(m)

            return 0

        lax.fori_loop(0, 6, first, 0)
        q_wait(0)
        pair_wait((0,))(0)
        pair_wait((0,))(1)
        u0, u1 = look(0), look(1)
        score(*u0, 0)
        score(*u1, 1)
        weigh(*u0, 0)

        def two(i, _):
            events(i)
            before, last, now, later = [look(2 * i + n) for n in (-2, -1, 0, 1)]
            score(*now, 0)
            weigh(*last, 1)
            gather(*before, 0)
            score(*later, 1)
            weigh(*now, 0)
            gather(*last, 1)
            return 0

        lax.fori_loop(1, LOOPS, two, 0)
        before, last = look(2 * LOOPS - 2), look(2 * LOOPS - 1)
        weigh(*last, 1)
        gather(*before, 0)
        gather(*last, 1)
        finish(3)

    for i in range(6):
        remote(att.at[:, columns(i)], att.at[:, columns(i)], a_send.at[0, i], o_recv.at[i], to_pair).wait_recv()

    w_copy.wait()
    width = o_ref.shape[1]
    part = width // PARTS

    def project(gy, gc, p):
        first = pl.multiple_of((gy * 2 + gc) * width + p * part, part)
        return jnp.dot(att[...], wv[:, pl.ds(first, part)], preferred_element_type=f32)

    def pair_copy(n, p):
        return remote(pair_out.at[n, p], pair_in.at[n, p], pair_send.at[n, p], pair_recv.at[n, p], to_pair)

    def cross_copy(p):
        return remote(cross_out.at[p], cross_in.at[p], cross_send.at[p], cross_recv.at[p], to_cross)

    for p in range(PARTS):
        pair_out[0, p] = project(1 - yh, 1 - c, p).astype(bf)
        pair_copy(0, p).start()
    for p in range(PARTS):
        own[p] = project(1 - yh, c, p)
        pair_copy(0, p).wait_recv()
        cross_out[p] = (own[p] + pair_in[0, p].astype(f32)).astype(bf)
        cross_copy(p).start()
    for p in range(PARTS):
        pair_out[1, p] = project(yh, 1 - c, p).astype(bf)
        pair_copy(1, p).start()
    for p in range(PARTS):
        own[p] = project(yh, c, p)
        pair_copy(1, p).wait_recv()
        own[p] += pair_in[1, p].astype(f32)
    for p in range(PARTS):
        cross_copy(p).wait_recv()
        o_ref[:, p * part : (p + 1) * part] = (own[p] + cross_in[p].astype(f32)).astype(bf)

    for p in range(PARTS):
        pair_copy(0, p).wait_send()
        pair_copy(1, p).wait_send()
        cross_copy(p).wait_send()

    def a_drain(m, _):
        a_sent((m + z) % 6, (2,))

        @pl.when(m >= 6 - WINDOW)
        def _():
            a_sent((m + z) % 6, (0, 1))

        return 0

    lax.fori_loop(0, 6, a_drain, 0)

    @pl.when(active)
    def _():
        def drain(b, _):
            for side in (0, 1):
                s = (b * 4 + x) * 2 + c
                to = to_right if side == 0 else to_left
                remote(kv.at[:, s], kv.at[:, s], x_send.at[side, b], x_recv.at[side, b], to).wait_send()
                remote(kv.at[side, s], kv.at[side, s], f_send.at[side, b], f_recv.at[side, b], to).wait_send()
            for rel in range(4):
                s = (b * 4 + (x + rel) % 4) * 2 + c
                remote(kv.at[:, s], kv.at[:, s], p_send.at[rel, b], p_recv.at[rel, b], to_pair).wait_send()

            @pl.when(jnp.logical_not(source_is_own(b)))
            def _():
                remote(
                    ot.at[b], att.at[:, columns(head)], o_send.at[b], o_recv.at[head],
                    device(b, x, c, yh, home_core),
                ).wait_send()

            return 0

        lax.fori_loop(0, 8, drain, 0)


def body(query, keys, values, out_weight, image_start):
    rows, depth = query.shape
    width = out_weight.shape[1] // lax.axis_size("head")
    part = width // PARTS
    bf, f32, dma, hd = jnp.bfloat16, jnp.float32, pltpu.SemaphoreType.DMA, HD
    return pl.pallas_call(
        kernel,
        out_shape=jax.ShapeDtypeStruct((rows, width), bf),
        in_specs=[pl.BlockSpec(memory_space=pl.ANY)] * 5,
        out_specs=pl.BlockSpec(memory_space=pltpu.VMEM),
        scratch_shapes=[
            pltpu.SMEM((3,), jnp.int32),
            pltpu.SMEM((len(TODO) * LOOPS,), jnp.int32),
            pltpu.VMEM((rows, depth), bf),
            pltpu.VMEM((rows, depth), bf),
            pltpu.VMEM((rows, depth), bf),
            pltpu.VMEM((6, hd, hd), bf),
            pltpu.VMEM((2, 64, hd, hd), bf),
            pltpu.VMEM((8, hd, hd), bf),
            pltpu.VMEM((4, hd + 16, 2 * hd), f32),
            pltpu.VMEM((4, 8, 2 * hd), f32),
            pltpu.VMEM((4, 8, 2 * hd), jnp.int32),
            pltpu.VMEM((8, hd, hd), bf),
            pltpu.VMEM((rows, depth), bf),
            pltpu.VMEM(out_weight.shape, bf),
            pltpu.VMEM((PARTS, rows, part), f32),
            pltpu.VMEM((2, PARTS, rows, part), bf),
            pltpu.VMEM((2, PARTS, rows, part), bf),
            pltpu.VMEM((PARTS, rows, part), bf),
            pltpu.VMEM((PARTS, rows, part), bf),
            pltpu.VMEM((2 * hd, 2 * hd), f32),
            pltpu.VMEM((2 * hd, 2 * hd), f32),
            pltpu.VMEM((2 * hd, 2 * hd), bf),
            pltpu.VMEM((2 * hd, 2 * hd), bf),
            pltpu.VMEM((8, 2 * hd), f32),
            pltpu.VMEM((8, 2 * hd), f32),
            dma((4,)), dma((3, 6)), dma((8,)), dma((8,)), dma((2, 8)), dma((2, 8)), dma((2, 8)), dma((2, 8)),
            dma((4, 8)), dma((4, 8)), dma((8,)), dma((6,)), dma,
            dma((2, PARTS)), dma((2, PARTS)), dma((PARTS,)), dma((PARTS,)),
        ],
        compiler_params=pltpu.CompilerParams(
            collective_id=0, has_side_effects=True, vmem_limit_bytes=48 * 1024 * 1024
        ),
    )(image_start, query, keys, values, out_weight)


def solution(mesh):
    placed = (P("seq", "head"), P("seq", "head"), P("seq", "head"), P("head", None), P())
    return jax.shard_map(body, mesh=mesh, in_specs=placed, out_specs=P("seq", "head"), check_vma=False)
```

```python
import jax
import jax.numpy as jnp
from jax import lax
from jax.experimental import pallas as pl
from jax.experimental.pallas import tpu as pltpu
from jax.sharding import PartitionSpec as P

MESH = pl.DeviceIdType.MESH
HD = 128
PATCHES = 1024
NEG = -1e30
SCALE = HD**-0.5
PARTS = 2

BY_QUERY = [(t, z) for t in range(4) for z in range(min(2 * t + 3, 8))]
BY_KEY = [(t, z) for z in range(8) for t in range(4) if z <= 2 * t + 2]
UNITS = [(t, z, 0) for t, z in BY_QUERY] + [(t, z, r) for t, z in BY_KEY for r in (3, 1)] + [(t, z, 2) for t, z in BY_QUERY]
LOOPS = len(UNITS) // 2
WINDOW = 4


def first_use(first, last):
    seen = {}
    for u in range(first, last):
        seen.setdefault(UNITS[u][1], u // 2)
    plan = {}
    for z, i in sorted(seen.items(), reverse=True):
        while i in plan:
            i -= 1
        plan[i] = z
    return {i: z for i, z in plan.items() if i > 0}


TODO = (
    {},
    {1: 0, 2: 1, 3: 2, 4: 3, 5: 4, 6: 5},
    {7: 0, 9: 1, 11: 2, 13: 3, 15: 4, 18: 5},
    first_use(0, 23),
    first_use(23, 69),
    first_use(69, 92),
    {1: 1, 4: 2, 7: 3},
    {37: 0, 40: 1, 43: 2},
)


def place():
    s, h = lax.axis_index("seq"), lax.axis_index("head")
    return s // 8, (s // 2) % 4, s % 2, h // 2, h % 2


def device(z, x, yl, yh, c):
    return ((z * 4 + x) * 2 + yl, yh * 2 + c)


def kernel(
    start_hbm, q_hbm, k_hbm, v_hbm, w_ref, o_ref,
    start_ref, todo, q_ref, k_ref, v_ref, vt, kv, qb, accs, ms, lims, ot, att, wv, own, pair_out, pair_in, cross_out, cross_in,
    s0, s1, p0, p1, al0, al1,
    in_sem, a_send, a_kv, a_q, x_send, x_recv, f_send, f_recv, p_send, p_recv, o_send, o_recv, w_sem,
    pair_send, pair_recv, cross_send, cross_recv,
):
    bf, f32 = jnp.bfloat16, jnp.float32
    z, x, yl, yh, c = place()
    couple = z // 2
    active = (z % 2 == 0) | (yl == couple % 2)
    home_core = z // 4
    head = 3 * (couple % 2) + jnp.where(z % 2 == 1, 2, yl)
    right, left = (x + 1) % 4, (x + 3) % 4
    opposite = (x + 2) % 4
    to_right = device(z, right, yl, yh, c)
    to_left = device(z, left, yl, yh, c)
    to_pair = device(z, x, yl, yh, 1 - c)
    to_cross = device(z, x, yl, 1 - yh, c)

    def remote(src, dst, send, recv, dev):
        return pltpu.make_async_remote_copy(src, dst, send, recv, device_id=dev, device_id_type=MESH)

    def worker(i):
        k, j = 2 * c + i // 3, i % 3
        extra = j == 2
        return 2 * k + jnp.where(extra, 1, 0), jnp.where(extra, k % 2, j)

    def is_own(i):
        wz, wyl = worker(i)
        return (wz == z) & (wyl == yl) & (yl == c)

    def source_is_own(zs):
        return (zs == z) & (yl == c) & (home_core == c)

    def columns(i):
        return pl.ds(pl.multiple_of(i * HD, HD), HD)

    copies = [
        pltpu.make_async_copy(src, dst, in_sem.at[n])
        for n, (src, dst) in enumerate(
            ((v_hbm, v_ref), (k_hbm, k_ref), (q_hbm, q_ref), (start_hbm, start_ref))
        )
    ]
    for copy in copies:
        copy.start()

    barrier = pltpu.get_barrier_semaphore()

    def greet(dev):
        pl.semaphore_signal(barrier, inc=1, device_id=dev, device_id_type=MESH)

    def greet_worker(i, _):
        wz, wyl = worker(i)

        @pl.when(jnp.logical_not(is_own(i)))
        def _():
            greet(device(wz, x, wyl, yh, yl))

        return 0

    @pl.when(active)
    def _():
        def greet_source(n, _):
            zs = (z + 4 + n) % 8

            @pl.when(jnp.logical_not(source_is_own(zs)))
            def _():
                greet(device(zs, x, c, yh, home_core))

            return 0

        lax.fori_loop(0, 8, greet_source, 0)
        greet(to_right)
        greet(to_left)

    lax.fori_loop(0, 6, greet_worker, 0)
    greet(to_pair)
    greet(to_cross)

    w_copy = pltpu.make_async_copy(w_ref, wv, w_sem)
    copies[0].wait()
    for i in range(6):
        vt[i] = v_ref[:, i * HD : (i + 1) * HD].T
    for copy in copies[1:]:
        copy.wait()
    w_copy.start()

    own_pair = ((yl == c) & (home_core == c) & active).astype(jnp.int32)
    expected = 8 + jnp.where(active, 10, 0) - 2 * own_pair
    pl.semaphore_wait(barrier, expected)

    slot = (z * 4 + x) * 2 + yl

    def pieces(i):
        return (
            (k_ref.at[:, columns(i)], kv.at[0, slot], a_kv.at[z]),
            (vt.at[i], kv.at[1, slot], a_kv.at[z]),
            (q_ref.at[:, columns(i)], qb.at[z], a_q.at[z]),
        )

    def a_copy(i, n):
        wz, wyl = worker(i)
        src, dst, sem = pieces(i)[n]
        return remote(src, dst, a_send.at[n, i], sem, device(wz, x, wyl, yh, yl))

    def a_start(i, ns):
        @pl.when(is_own(i))
        def _():
            for n in ns:
                src, dst, sem = pieces(i)[n]
                pltpu.make_async_copy(src, dst, sem).start()

        @pl.when(jnp.logical_not(is_own(i)))
        def _():
            for n in ns:
                a_copy(i, n).start()

    def a_sent(i, ns):
        @pl.when(jnp.logical_not(is_own(i)))
        def _():
            for n in ns:
                a_copy(i, n).wait_send()

    def a_round(m):
        @pl.when(m < 6)
        def _():
            @pl.when(m >= WINDOW)
            def _():
                a_sent((m - WINDOW + z) % 6, (0, 1))

            a_start((m + z) % 6, (0, 1))

        @pl.when(m == 8)
        def _():
            def all_q(n, _):
                a_start((n + z) % 6, (2,))
                return 0

            lax.fori_loop(0, 6, all_q, 0)

    @pl.when(jnp.logical_not(active))
    def _():
        def step(m, _):
            a_round(m)
            return 0

        lax.fori_loop(0, 9, step, 0)

    @pl.when(active)
    def _():
        def at(zk, xk, w):
            return (zk * 4 + xk) * 2 + w

        def x_copy(side, b):
            s = at(b, x, c)
            return remote(
                kv.at[:, s], kv.at[:, s], x_send.at[side, b], x_recv.at[side, b], to_right if side == 0 else to_left
            )

        def x_wait(side, b):
            s = at(b, left if side == 0 else right, c)
            remote(
                kv.at[:, s], kv.at[:, s], x_send.at[side, b], x_recv.at[side, b], to_right if side == 0 else to_left
            ).wait_recv()

        def f_copy(side, b):
            s = at(b, left if side == 0 else right, c)
            return remote(
                kv.at[side, s], kv.at[side, s], f_send.at[side, b], f_recv.at[side, b],
                to_right if side == 0 else to_left,
            )

        def f_wait(side, b):
            s = at(b, opposite, c)
            remote(
                kv.at[side, s], kv.at[side, s], f_send.at[side, b], f_recv.at[side, b],
                to_right if side == 0 else to_left,
            ).wait_recv()

        def p_copy(rel, b, w):
            s = at(b, (x + rel) % 4, w)
            return remote(kv.at[:, s], kv.at[:, s], p_send.at[rel, b], p_recv.at[rel, b], to_pair)

        def o_copy(zq):
            return remote(
                ot.at[zq], att.at[:, columns(head)], o_send.at[zq], o_recv.at[head],
                device(zq, x, c, yh, home_core),
            )

        def own_step(b):
            s = at(b, x, c)
            remote(kv.at[:, s], kv.at[:, s], x_send.at[0, b], a_kv.at[b], to_pair).wait_recv()
            x_copy(0, b).start()
            x_copy(1, b).start()
            p_copy(0, b, c).start()

        def side_step(b):
            x_wait(0, b)
            f_copy(0, b).start()
            p_copy(3, b, c).start()
            x_wait(1, b)
            f_copy(1, b).start()
            p_copy(1, b, c).start()

        def far_step(b):
            f_wait(0, b)
            f_wait(1, b)
            p_copy(2, b, c).start()

        def q_wait(t):
            for b in (2 * t, 2 * t + 1):
                remote(qb.at[b], qb.at[b], x_send.at[0, b], a_q.at[b], to_pair).wait_recv()

        scores, weights, scales = (s0, s1), (p0, p1), (al0, al1)
        rows = lax.broadcasted_iota(jnp.int32, (2 * HD, 2 * HD), 0)
        ones = jnp.ones((16, 2 * HD), bf)

        def score(t, b, n):
            k = kv[0, pl.ds(b, 2)].reshape(2 * HD, HD)
            q = qb[pl.ds(2 * t, 2)].reshape(2 * HD, HD)
            scores[n][...] = lax.dot_general(k, q, (((1,), (1,)), ((), ())), preferred_element_type=f32)

        def weigh(t, b, n):
            sc = jnp.where(rows <= lims[t, 0:1] - b * HD, scores[n][...], NEG)
            m = ms[t, 0:1]
            m_new = jnp.maximum(m, jnp.max(sc, axis=0, keepdims=True))
            weights[n][...] = jnp.exp((sc - m_new) * SCALE).astype(bf)
            scales[n][...] = jnp.broadcast_to(jnp.exp((m - m_new) * SCALE), (8, 2 * HD))
            ms[t, 0:1] = m_new

        def gather(t, b, n):
            v = jnp.concatenate([jnp.concatenate([kv[1, b], kv[1, b + 1]], axis=1), ones], axis=0)
            accs[t] = accs[t] * scales[n][0:1] + jnp.dot(v, weights[n][...], preferred_element_type=f32)

        def finish(t):
            total = accs[t]
            done = total[:HD] * (1.0 / total[HD : HD + 1])
            for j in range(2):
                zq = 2 * t + j
                ot[zq] = done[:, j * HD : (j + 1) * HD].T.astype(bf)

                @pl.when(source_is_own(zq))
                def _():
                    pltpu.make_async_copy(ot.at[zq], att.at[:, columns(head)], o_recv.at[head]).start()

                @pl.when(jnp.logical_not(source_is_own(zq)))
                def _():
                    o_copy(zq).start()

        def pair_wait(rels):
            def run(b):
                for rel in rels:
                    p_copy(rel, b, 1 - c).wait_recv()

            return run

        def in_round(step):
            def run(m):
                b = (head + 12 - m) % 6
                step(b)

                @pl.when(b < 2)
                def _():
                    step(b + 6)

            return run

        actions = (in_round(side_step), in_round(far_step), pair_wait((0,)), pair_wait((3, 1)), pair_wait((2,)), q_wait, finish)

        def events(i):
            @pl.when(todo[i] >= 0)
            def _():
                for k, action in enumerate(actions):
                    value = todo[(k + 1) * LOOPS + i]

                    @pl.when(value >= 0)
                    def _():
                        action(value)

        def steps(u, marks):
            n = jnp.int32(0)
            for mark in marks:
                n = n + (u >= mark).astype(jnp.int32)
            return n

        def unit(u):
            u = jnp.asarray(u, jnp.int32)
            by_query = (u < 23) | (u >= 69)
            v = jnp.where(u < 23, u, jnp.where(u < 69, (u - 23) // 2, u - 69))
            tq = steps(v, (3, 8, 15))
            zq = v - tq * (tq + 2)
            zk = steps(v, (4, 8, 12, 15, 18, 20, 22))
            skipped = steps(v, (15, 20, 22))
            low = steps(zk, (3, 5, 7))
            begin = 4 * zk - steps(zk, (4, 5, 6, 6, 7, 7))
            tk = low + v - begin
            rel = jnp.where(u < 23, 0, jnp.where(u >= 69, 2, jnp.where((u - 23) % 2 == 0, 3, 1)))
            t = jnp.where(by_query, tq, tk)
            zz = jnp.where(by_query, zq, zk)
            return t, zz, rel

        def look(u):
            t, zz, rel = unit(u)
            return t, at(zz, (x + rel) % 4, 0)

        for m in range(WINDOW - 1):
            a_round(jnp.int32(m))

        def clear(n, _):
            for k in range(len(TODO)):
                todo[k * LOOPS + n] = -1
            return 0

        lax.fori_loop(0, LOOPS, clear, 0)
        for k, plan in enumerate(TODO):
            for i, value in plan.items():
                todo[k * LOOPS + i] = value
                todo[i] = 0
        lanes = lax.broadcasted_iota(jnp.int32, (1, 2 * HD), 1)
        for t in range(4):
            zq = 2 * t + lanes // HD
            pos = ((zq * 4 + x) * 2 + c) * HD + lanes % HD
            lim = pos
            for n in range(3):
                first = start_ref[n]
                lim = jnp.where((pos >= first) & (pos < first + PATCHES), first + (PATCHES - 1), lim)
            lims[t] = jnp.broadcast_to(lim, (8, 2 * HD))
        ms[...] = jnp.full_like(ms, NEG)
        accs[...] = jnp.zeros_like(accs)

        def first(m, _):
            a_round(m + (WINDOW - 1))
            in_round(own_step)(m)

            return 0

        lax.fori_loop(0, 6, first, 0)
        q_wait(0)
        pair_wait((0,))(0)
        pair_wait((0,))(1)
        u0, u1 = look(0), look(1)
        score(*u0, 0)
        score(*u1, 1)
        weigh(*u0, 0)

        def two(i, _):
            events(i)
            before, last, now, later = [look(2 * i + n) for n in (-2, -1, 0, 1)]
            score(*now, 0)
            weigh(*last, 1)
            gather(*before, 0)
            score(*later, 1)
            weigh(*now, 0)
            gather(*last, 1)
            return 0

        lax.fori_loop(1, LOOPS, two, 0)
        before, last = look(2 * LOOPS - 2), look(2 * LOOPS - 1)
        weigh(*last, 1)
        gather(*before, 0)
        gather(*last, 1)
        finish(3)

    for i in range(6):
        remote(att.at[:, columns(i)], att.at[:, columns(i)], a_send.at[0, i], o_recv.at[i], to_pair).wait_recv()

    w_copy.wait()
    width = o_ref.shape[1]
    part = width // PARTS

    def project(gy, gc, p):
        first = pl.multiple_of((gy * 2 + gc) * width + p * part, part)
        return jnp.dot(att[...], wv[:, pl.ds(first, part)], preferred_element_type=f32)

    def pair_copy(n, p):
        return remote(pair_out.at[n, p], pair_in.at[n, p], pair_send.at[n, p], pair_recv.at[n, p], to_pair)

    def cross_copy(p):
        return remote(cross_out.at[p], cross_in.at[p], cross_send.at[p], cross_recv.at[p], to_cross)

    for p in range(PARTS):
        pair_out[0, p] = project(1 - yh, 1 - c, p).astype(bf)
        pair_copy(0, p).start()
    for p in range(PARTS):
        own[p] = project(1 - yh, c, p)
        pair_copy(0, p).wait_recv()
        cross_out[p] = (own[p] + pair_in[0, p].astype(f32)).astype(bf)
        cross_copy(p).start()
    for p in range(PARTS):
        pair_out[1, p] = project(yh, 1 - c, p).astype(bf)
        pair_copy(1, p).start()
    for p in range(PARTS):
        own[p] = project(yh, c, p)
        pair_copy(1, p).wait_recv()
        own[p] += pair_in[1, p].astype(f32)
    for p in range(PARTS):
        cross_copy(p).wait_recv()
        o_ref[:, p * part : (p + 1) * part] = (own[p] + cross_in[p].astype(f32)).astype(bf)

    for p in range(PARTS):
        pair_copy(0, p).wait_send()
        pair_copy(1, p).wait_send()
        cross_copy(p).wait_send()

    def a_drain(m, _):
        a_sent((m + z) % 6, (2,))

        @pl.when(m >= 6 - WINDOW)
        def _():
            a_sent((m + z) % 6, (0, 1))

        return 0

    lax.fori_loop(0, 6, a_drain, 0)

    @pl.when(active)
    def _():
        def drain(b, _):
            for side in (0, 1):
                s = (b * 4 + x) * 2 + c
                to = to_right if side == 0 else to_left
                remote(kv.at[:, s], kv.at[:, s], x_send.at[side, b], x_recv.at[side, b], to).wait_send()
                remote(kv.at[side, s], kv.at[side, s], f_send.at[side, b], f_recv.at[side, b], to).wait_send()
            for rel in range(4):
                s = (b * 4 + (x + rel) % 4) * 2 + c
                remote(kv.at[:, s], kv.at[:, s], p_send.at[rel, b], p_recv.at[rel, b], to_pair).wait_send()

            @pl.when(jnp.logical_not(source_is_own(b)))
            def _():
                remote(
                    ot.at[b], att.at[:, columns(head)], o_send.at[b], o_recv.at[head],
                    device(b, x, c, yh, home_core),
                ).wait_send()

            return 0

        lax.fori_loop(0, 8, drain, 0)


def body(query, keys, values, out_weight, image_start):
    rows, depth = query.shape
    width = out_weight.shape[1] // lax.axis_size("head")
    part = width // PARTS
    bf, f32, dma, hd = jnp.bfloat16, jnp.float32, pltpu.SemaphoreType.DMA, HD
    return pl.pallas_call(
        kernel,
        out_shape=jax.ShapeDtypeStruct((rows, width), bf),
        in_specs=[pl.BlockSpec(memory_space=pl.ANY)] * 5,
        out_specs=pl.BlockSpec(memory_space=pltpu.VMEM),
        scratch_shapes=[
            pltpu.SMEM((3,), jnp.int32),
            pltpu.SMEM((len(TODO) * LOOPS,), jnp.int32),
            pltpu.VMEM((rows, depth), bf),
            pltpu.VMEM((rows, depth), bf),
            pltpu.VMEM((rows, depth), bf),
            pltpu.VMEM((6, hd, hd), bf),
            pltpu.VMEM((2, 64, hd, hd), bf),
            pltpu.VMEM((8, hd, hd), bf),
            pltpu.VMEM((4, hd + 16, 2 * hd), f32),
            pltpu.VMEM((4, 8, 2 * hd), f32),
            pltpu.VMEM((4, 8, 2 * hd), jnp.int32),
            pltpu.VMEM((8, hd, hd), bf),
            pltpu.VMEM((rows, depth), bf),
            pltpu.VMEM(out_weight.shape, bf),
            pltpu.VMEM((PARTS, rows, part), f32),
            pltpu.VMEM((2, PARTS, rows, part), bf),
            pltpu.VMEM((2, PARTS, rows, part), bf),
            pltpu.VMEM((PARTS, rows, part), bf),
            pltpu.VMEM((PARTS, rows, part), bf),
            pltpu.VMEM((2 * hd, 2 * hd), f32),
            pltpu.VMEM((2 * hd, 2 * hd), f32),
            pltpu.VMEM((2 * hd, 2 * hd), bf),
            pltpu.VMEM((2 * hd, 2 * hd), bf),
            pltpu.VMEM((8, 2 * hd), f32),
            pltpu.VMEM((8, 2 * hd), f32),
            dma((4,)), dma((3, 6)), dma((8,)), dma((8,)), dma((2, 8)), dma((2, 8)), dma((2, 8)), dma((2, 8)),
            dma((4, 8)), dma((4, 8)), dma((8,)), dma((6,)), dma,
            dma((2, PARTS)), dma((2, PARTS)), dma((PARTS,)), dma((PARTS,)),
        ],
        compiler_params=pltpu.CompilerParams(
            collective_id=0, has_side_effects=True, vmem_limit_bytes=48 * 1024 * 1024
        ),
    )(image_start, query, keys, values, out_weight)


def solution(mesh):
    placed = (P("seq", "head"), P("seq", "head"), P("seq", "head"), P("head", None), P())
    return jax.shard_map(body, mesh=mesh, in_specs=placed, out_specs=P("seq", "head"), check_vma=False)
```
